32 devices in a mesh: sample: 2 (over x), space: 16 (over z, y, core).
Axes of the slice: x: 2, y: 2, z: 4, core: 2. Of those that a mesh axis runs over, the one named last changes fastest.
Arguments:
- features: bfloat16 [2, 4, 128, 128, 128], P('sample', None, 'space'), parts along dimension 0, may hold values from -6 to 6
- log_perm: float32 [2, 128, 128, 128], P('sample', 'space'), parts along dimension 0, may hold values from -1.5 to 1.5
- well_cells: int32 [2, 32], P('sample'), parts along dimension 0, may hold values from 0 to 2097151
- well_rates: float32 [2, 32], P('sample'), parts along dimension 0, may hold values from 10 to 70
- lift_in: bfloat16 [5, 128], replicated, may hold values from -2.5 to 2.5
- lift_out: bfloat16 [128, 32], replicated, may hold values from -0.5 to 0.5
- spec_weight: bfloat16 [2, 1024, 32, 2048], P(None, 'space'), may hold values from -2 to 2
- point_weight: bfloat16 [2, 32, 32], replicated, may hold values from -1 to 1
- dec_in: bfloat16 [32, 64], replicated, may hold values from -1 to 1
- dec_out: bfloat16 [64, 2], replicated, may hold values from -0.75 to 0.75
Outputs:
- states: float32 [2, 2, 128, 128, 128], P('sample', None, 'space'), parts along dimension 0
- residual: float32 [2, 128, 128, 128], P('sample', 'space'), parts along dimension 0
The draws below stay inside these ranges and needn't reach their ends.
There are 2 independent parts, one for each index of `sample`. The reference program is written for one: setup_inputs(seed, part) draws one part's arguments, and reference() takes and returns one part's arrays. A program takes and returns all parts, laid end to end along the dimension named above; an argument that names none is the same for every part. Nothing has to cross between parts.
Inputs may be any that keep to these rules, and one draw needn't show every extreme that they name: `well_cells`: cells of the sample's grid; several wells may share a cell.
All inputs are finite; a program needn't handle non-finite values.
Results may differ from the reference program's by a relative error of at most 0.03.
Values may be sent and summed in bfloat16 or wider, within the bound.
A program may use at most 192 MiB of HBM per device.

```python
import math
import jax
import jax.numpy as jnp
from jax import lax

BATCH = 1
NX = 128
NY = 128
NZ = 128
MX = 32
MY = 32
MZ = 32
C = 32
FIN = 4
LIFT = 128
DEC = 64
LAYERS = 2
WELLS = 32


def touch_ends(drawn, key, least, top_value):
    longest = drawn.shape.index(max(drawn.shape))
    spots = []
    for shift in (0, 1):
        where = [jax.random.randint(jax.random.fold_in(key, axis), (), 0, length) for axis, length in enumerate(drawn.shape)]
        where[longest] = (where[longest] + shift) % drawn.shape[longest]
        spots.append(tuple(where))
    return drawn.at[spots[0]].set(least).at[spots[1]].set(top_value)


def level_of(stream_key, extent, split, least, largest):
    def one(dim, parts):
        draws = jax.random.uniform(jax.random.fold_in(jax.random.fold_in(stream_key, 6), dim), (parts,), jnp.float32, least / len(split), largest / len(split))
        return jnp.repeat(jnp.exp(draws), extent[dim] // parts).reshape((-1,) + (1,) * (len(extent) - dim - 1))

    gain = one(*split[0])
    for cut in split[1:]:
        gain = gain * one(*cut)
    return gain


def bell_draw(rng, dims, scale, bound, pieces=(), held_as=jnp.bfloat16):
    level = level_of(rng, dims, pieces, -0.22, 0.18) if pieces else 1.0
    result = jax.random.normal(rng, dims, jnp.float32) * scale * level
    return jnp.minimum(jnp.maximum(result, -bound), bound).astype(held_as)


def setup_inputs(seed: int = 0, part: int = 0) -> dict:
    splits = jax.random.split(jax.random.key(seed), 11)
    own_keys = jax.random.split(jax.random.fold_in(splits[10], part), 11)
    return {
        "features": bell_draw(own_keys[0], (BATCH, FIN, NX, NY, NZ), 1.0, 6.0, ((2, 16),)),
        "log_perm": jnp.clip(jax.random.uniform(own_keys[1], (BATCH, NX, NY, NZ), jnp.float32, -1.5, 1.5) * level_of(own_keys[1], (BATCH, NX, NY, NZ), ((1, 16),), -0.4, 0.0), -1.5, 1.5),
        "well_cells": touch_ends(jax.random.randint(own_keys[2], (BATCH, WELLS), 0, NX * NY * NZ), jax.random.fold_in(own_keys[2], 1), 0, (NX * NY * NZ) - 1).astype(jnp.int32),
        "well_rates": jnp.clip(jax.random.uniform(own_keys[3], (BATCH, WELLS), jnp.float32, 10.0, 70.0), 10.0, 70.0),
        "lift_in": bell_draw(splits[4], (FIN + 1, LIFT), (FIN + 1) ** -0.5, 2.5),
        "lift_out": bell_draw(splits[5], (LIFT, C), LIFT ** -0.5, 0.5),
        "spec_weight": bell_draw(splits[6], (LAYERS, MY * MZ, C, MX * 2 * C), (C // 4) ** -0.5, 2.0, ((1, 16),)),
        "point_weight": bell_draw(splits[7], (LAYERS, C, C), C ** -0.5, 1.0),
        "dec_in": bell_draw(splits[8], (C, DEC), C ** -0.5, 1.0),
        "dec_out": bell_draw(splits[9], (DEC, 2), DEC ** -0.5, 0.75),
    }


def freq_table(length, kept, one_sided):
    indices = jnp.arange(kept, dtype=jnp.int32)
    if one_sided:
        return indices
    return jnp.where(indices < kept // 2, indices, length - kept + indices).astype(jnp.int32)

def wave_parts(length, kept, one_sided):
    freqs = freq_table(length, kept, one_sided)
    places = jnp.arange(length, dtype=jnp.int32)
    phase_turns = freqs[:, None] * places[None, :] % length
    angles = phase_turns.astype(jnp.float32) * (2.0 * math.pi / length)
    norm_scale = 1.0 / math.sqrt(length)
    return (jnp.cos(angles) * norm_scale, jnp.sin(angles) * norm_scale)

def forward_table(length, kept):
    cosine_vals, sine_vals = wave_parts(length, kept, False)
    return jnp.stack([jnp.stack([cosine_vals.T, -sine_vals.T], 1), jnp.stack([sine_vals.T, cosine_vals.T], 1)], 1).astype(jnp.bfloat16)

def inverse_table(length, kept):
    cosine_vals, sine_vals = wave_parts(length, kept, False)
    return jnp.stack([jnp.stack([cosine_vals, sine_vals], 1), jnp.stack([-sine_vals, cosine_vals], 1)], 1).astype(jnp.bfloat16)

def z_tables():
    cosine_vals, sine_vals = wave_parts(NZ, MZ, True)
    weights_k = jnp.where(jnp.arange(MZ) == 0, 1.0, 2.0).astype(jnp.float32)[:, None]
    z_forward = jnp.concatenate([cosine_vals.T, -sine_vals.T], 1).astype(jnp.bfloat16)
    z_inverse = jnp.concatenate([weights_k * cosine_vals, -weights_k * sine_vals], 0).astype(jnp.bfloat16)
    return (z_forward, z_inverse)

def gelu_tanh(values):
    return jax.nn.gelu(values, approximate=True)

def face_term(cond_a, cond_b, press_a, press_b):
    return 2.0 * cond_a * cond_b / (cond_a + cond_b) * (press_a - press_b)

def fourier_layer(hidden_state, weight_slice, point_slice, tables):
    z_forward, z_inverse, y_forward, y_inverse, x_forward, x_inverse = tables
    zspec = jnp.dot(hidden_state.reshape(-1, NZ), z_forward, preferred_element_type=jnp.float32)
    zspec = zspec.astype(jnp.bfloat16).reshape(NX, C, NY, 2, MZ)
    yz_spec = jnp.einsum('xcypk,ypqj->xcqjk', zspec.astype(jnp.float32), y_forward.astype(jnp.float32))
    yz_spec = yz_spec.astype(jnp.bfloat16).reshape(NX, C, 2, MY * MZ)
    spectrum = jnp.einsum('xcpm,xpqi->cqim', yz_spec.astype(jnp.float32), x_forward.astype(jnp.float32)).astype(jnp.bfloat16)
    mode_weights = weight_slice.reshape(MY * MZ, C, MX, 2, C).astype(jnp.float32)
    products = jnp.einsum('cqim,mcipo->imqpo', spectrum.astype(jnp.float32), mode_weights)
    real_part = products[:, :, 0, 0] - products[:, :, 1, 1]
    imag_part = products[:, :, 0, 1] + products[:, :, 1, 0]
    mixed_modes = jnp.stack([real_part, imag_part], 2).astype(jnp.bfloat16)
    back_field = jnp.einsum('imqo,iqpx->xopm', mixed_modes.astype(jnp.float32), x_inverse.astype(jnp.float32))
    back_field = back_field.astype(jnp.bfloat16).reshape(NX, C, 2, MY, MZ)
    y_back = jnp.einsum('xcqjk,jqpy->xcypk', back_field.astype(jnp.float32), y_inverse.astype(jnp.float32)).astype(jnp.bfloat16)
    spectral = jnp.dot(y_back.reshape(-1, 2 * MZ), z_inverse, preferred_element_type=jnp.float32).reshape(NX, C, NY * NZ)
    local_term = jnp.einsum('xcn,co->xon', hidden_state.astype(jnp.float32), point_slice.astype(jnp.float32))
    return gelu_tanh(spectral + local_term).astype(jnp.bfloat16)

def reference(features, log_perm, well_cells, well_rates, lift_in, lift_out, spec_weight, point_weight, dec_in, dec_out):
    z_forward, z_inverse = z_tables()
    tables = (z_forward, z_inverse, forward_table(NY, MY), inverse_table(NY, MY), forward_table(NX, MX), inverse_table(NX, MX))
    plane_size = NY * NZ
    all_states = []
    all_resid = []

    def lift_plane(plane_in):
        lift_hidden = jnp.dot(lift_in.T, plane_in, preferred_element_type=jnp.float32)
        lifted = gelu_tanh(lift_hidden).astype(jnp.bfloat16)
        return jnp.dot(lift_out.T, lifted, preferred_element_type=jnp.float32).astype(jnp.bfloat16)

    def decode_plane(plane_state):
        decoded = gelu_tanh(jnp.dot(dec_in.T, plane_state, preferred_element_type=jnp.float32)).astype(jnp.bfloat16)
        decoded_out = jnp.dot(dec_out.T, decoded, preferred_element_type=jnp.float32)
        return jnp.stack([decoded_out[0], jax.nn.sigmoid(decoded_out[1])], 0)
    for sample_idx in range(BATCH):
        perm_b = log_perm[sample_idx].astype(jnp.bfloat16)
        feature_planes = features[sample_idx].transpose(1, 0, 2, 3).reshape(NX, FIN, plane_size)
        lift_input = jnp.concatenate([feature_planes, perm_b.reshape(NX, 1, plane_size)], 1)
        hidden_state = lax.map(lift_plane, lift_input)
        for layer_idx in range(LAYERS):
            hidden_state = fourier_layer(hidden_state, spec_weight[layer_idx], point_weight[layer_idx], tables)
        plane_states = lax.map(decode_plane, hidden_state)
        states = plane_states.transpose(1, 0, 2).reshape(2, NX, NY, NZ)
        pressure = states[0]
        saturation = states[1]
        conduct = jnp.exp(log_perm[sample_idx]) * (saturation * saturation + 0.5 * (1.0 - saturation) * (1.0 - saturation))
        pad_cond = jnp.pad(conduct, 1)
        pad_press = jnp.pad(pressure, 1)
        flux_sum = face_term(conduct, pad_cond[2:, 1:-1, 1:-1], pressure, pad_press[2:, 1:-1, 1:-1])
        flux_sum = flux_sum + face_term(conduct, pad_cond[:-2, 1:-1, 1:-1], pressure, pad_press[:-2, 1:-1, 1:-1])
        flux_sum = flux_sum + face_term(conduct, pad_cond[1:-1, 2:, 1:-1], pressure, pad_press[1:-1, 2:, 1:-1])
        flux_sum = flux_sum + face_term(conduct, pad_cond[1:-1, :-2, 1:-1], pressure, pad_press[1:-1, :-2, 1:-1])
        flux_sum = flux_sum + face_term(conduct, pad_cond[1:-1, 1:-1, 2:], pressure, pad_press[1:-1, 1:-1, 2:])
        flux_sum = flux_sum + face_term(conduct, pad_cond[1:-1, 1:-1, :-2], pressure, pad_press[1:-1, 1:-1, :-2])
        source = jnp.zeros((NX * NY * NZ,), jnp.float32).at[well_cells[sample_idx]].add(well_rates[sample_idx])
        all_states.append(states)
        all_resid.append(flux_sum - source.reshape(NX, NY, NZ))
    return (jnp.stack(all_states, 0), jnp.stack(all_resid, 0))
```

```python
import math

import jax
import jax.numpy as jnp
import numpy as np
from jax import lax
from jax.experimental import pallas as pl
from jax.experimental.pallas import tpu as pltpu
from jax.sharding import PartitionSpec as P

NX = 128
NY = 128
NZ = 128
MX = 32
MY = 32
MZ = 32
C = 32
FIN = 4
LAYERS = 2
WELLS = 32


def padded_2(block, sides, width):
    for axis, dim in sides:
        count = lax.axis_size(axis)
        forward = [(i, i + 1) for i in range(count - 1)]
        backward = [(target, source) for source, target in forward]
        low = lax.ppermute(
            lax.slice_in_dim(block, block.shape[dim] - width, None, axis=dim), axis, forward
        )
        high = lax.ppermute(lax.slice_in_dim(block, 0, width, axis=dim), axis, backward)
        block = jnp.concatenate([low, block, high], axis=dim)
    return block


def freq_table(length, kept, one_sided):
    indices = jnp.arange(kept, dtype=jnp.int32)
    if one_sided:
        return indices
    return jnp.where(indices < kept // 2, indices, length - kept + indices)


def wave_parts(length, kept, one_sided):
    freqs = freq_table(length, kept, one_sided)
    places = jnp.arange(length, dtype=jnp.int32)
    phase_turns = freqs[:, None] * places[None, :] % length
    angles = phase_turns.astype(jnp.float32) * (2.0 * math.pi / length)
    norm_scale = 1.0 / math.sqrt(length)
    return (jnp.cos(angles) * norm_scale, jnp.sin(angles) * norm_scale)


def forward_table(length, kept):
    cosine_vals, sine_vals = wave_parts(length, kept, False)
    return jnp.stack(
        [jnp.stack([cosine_vals.T, -sine_vals.T], 1), jnp.stack([sine_vals.T, cosine_vals.T], 1)], 1
    ).astype(jnp.bfloat16)


def inverse_table(length, kept):
    cosine_vals, sine_vals = wave_parts(length, kept, False)
    return jnp.stack(
        [jnp.stack([cosine_vals, sine_vals], 1), jnp.stack([-sine_vals, cosine_vals], 1)], 1
    ).astype(jnp.bfloat16)


def z_tables():
    cosine_vals, sine_vals = wave_parts(NZ, MZ, True)
    weights_k = jnp.where(jnp.arange(MZ) == 0, 1.0, 2.0).astype(jnp.float32)[:, None]
    z_forward = jnp.concatenate([cosine_vals.T, -sine_vals.T], 1).astype(jnp.bfloat16)
    z_inverse = jnp.concatenate([weights_k * cosine_vals, -weights_k * sine_vals], 0).astype(
        jnp.bfloat16
    )
    return (z_forward, z_inverse)


def gelu_tanh(values):
    return jax.nn.gelu(values, approximate=True)


def face_term(cond_a, cond_b, press_a, press_b):
    return 2.0 * cond_a * cond_b / (cond_a + cond_b) * (press_a - press_b)


def mobility_of(saturation, log_values):
    return jnp.exp(log_values) * (
        saturation * saturation + 0.5 * (1.0 - saturation) * (1.0 - saturation)
    )


def darcy(pressure, conduct, well_cells, well_rates):
    batches, planes = pressure.shape[0], pressure.shape[1]
    space_index = lax.axis_index("space")
    pad_cond = jnp.pad(conduct, ((0, 0), (0, 0), (1, 1), (1, 1)))
    pad_press = jnp.pad(pressure, ((0, 0), (0, 0), (1, 1), (1, 1)))
    flux_sum = face_term(conduct, pad_cond[:, :, 2:, 1:-1], pressure, pad_press[:, :, 2:, 1:-1])
    flux_sum = flux_sum + face_term(
        conduct, pad_cond[:, :, :-2, 1:-1], pressure, pad_press[:, :, :-2, 1:-1]
    )
    flux_sum = flux_sum + face_term(
        conduct, pad_cond[:, :, 1:-1, 2:], pressure, pad_press[:, :, 1:-1, 2:]
    )
    flux_sum = flux_sum + face_term(
        conduct, pad_cond[:, :, 1:-1, :-2], pressure, pad_press[:, :, 1:-1, :-2]
    )
    fields = jnp.stack([pressure, conduct], 1)
    padded = padded_2(fields.astype(jnp.bfloat16), (("space", 2),), 1).astype(fields.dtype)
    press_low = padded[:, 0, 0]
    press_high = padded[:, 0, -1]
    cond_low = padded[:, 1, 0]
    cond_high = padded[:, 1, -1]
    press_below = jnp.concatenate([press_low[:, None], pressure[:, :-1]], 1)
    cond_below = jnp.concatenate([cond_low[:, None], conduct[:, :-1]], 1)
    press_above = jnp.concatenate([pressure[:, 1:], press_high[:, None]], 1)
    cond_above = jnp.concatenate([conduct[:, 1:], cond_high[:, None]], 1)
    lower_terms = face_term(conduct, cond_below, pressure, press_below)
    upper_terms = face_term(conduct, cond_above, pressure, press_above)
    flux_sum = flux_sum + lower_terms + upper_terms
    well_x = well_cells // (NY * NZ) - space_index * planes
    well_y = well_cells // NZ % NY
    well_z = well_cells % NZ
    onehot_x = (well_x[:, :, None] == jnp.arange(planes, dtype=jnp.int32)[None, None, :]).astype(
        jnp.float32
    ) * well_rates[:, :, None]
    onehot_y = (well_y[:, :, None] == jnp.arange(NY, dtype=jnp.int32)[None, None, :]).astype(
        jnp.float32
    )
    onehot_z = (well_z[:, :, None] == jnp.arange(NZ, dtype=jnp.int32)[None, None, :]).astype(
        jnp.float32
    )
    plane_rows = (onehot_x[:, :, :, None] * onehot_y[:, :, None, :]).reshape(
        batches, WELLS, planes * NY
    )
    source = jnp.einsum(
        "bwa,bwz->baz", plane_rows, onehot_z, precision=lax.Precision.HIGHEST
    ).reshape(batches, planes, NY, NZ)
    return flux_sum - source


def local_general(
    features,
    log_perm,
    well_cells,
    well_rates,
    lift_in,
    lift_out,
    spec_weight,
    point_weight,
    dec_in,
    dec_out,
):
    batches = features.shape[0]
    planes = features.shape[2]
    space_index = lax.axis_index("space")
    block = spec_weight.shape[1]
    cell_count = planes * NY * NZ
    z_forward, z_inverse = z_tables()
    y_forward = forward_table(NY, MY)
    y_inverse = inverse_table(NY, MY)
    x_forward = forward_table(NX, MX)
    x_inverse = inverse_table(NX, MX)
    perm_b = log_perm.astype(jnp.bfloat16).reshape(batches, 1, cell_count)
    lift_input = jnp.concatenate([features.reshape(batches, FIN, cell_count), perm_b], 1)
    lift_hidden = jnp.einsum("bfn,fh->bhn", lift_input, lift_in, preferred_element_type=jnp.float32)
    lifted = gelu_tanh(lift_hidden).astype(jnp.bfloat16)
    hidden_state = jnp.einsum(
        "bhn,hc->bcn", lifted, lift_out, preferred_element_type=jnp.float32
    ).astype(jnp.bfloat16)
    for layer_idx in range(LAYERS):
        zspec = jnp.dot(hidden_state.reshape(-1, NZ), z_forward, preferred_element_type=jnp.float32)
        zspec = zspec.astype(jnp.bfloat16).reshape(batches * C * planes, NY, 2, MZ)
        yz_spec = jnp.einsum(
            "aypk,ypqj->aqjk", zspec, y_forward, preferred_element_type=jnp.float32
        )
        yz_spec = yz_spec.astype(jnp.bfloat16).reshape(batches, C, planes, 2, MY * MZ)
        mode_weights = spec_weight[layer_idx].reshape(block, C, MX, 2, C)
        spectrum = jnp.einsum(
            "bcxpm,xpqi->bcqim",
            lax.all_to_all(yz_spec, "space", split_axis=4, concat_axis=2, tiled=True),
            x_forward,
            preferred_element_type=jnp.float32,
        ).astype(jnp.bfloat16)
        products = jnp.einsum(
            "bcqim,mcipo->bimqpo", spectrum, mode_weights, preferred_element_type=jnp.float32
        )
        real_part = products[:, :, :, 0, 0] - products[:, :, :, 1, 1]
        imag_part = products[:, :, :, 0, 1] + products[:, :, :, 1, 0]
        mixed_modes = jnp.stack([real_part, imag_part], 3).astype(jnp.bfloat16)
        back_field = jnp.einsum(
            "bimqo,iqpx->boxpm", mixed_modes, x_inverse, preferred_element_type=jnp.float32
        ).astype(jnp.bfloat16)
        returned = lax.all_to_all(back_field, "space", split_axis=2, concat_axis=4, tiled=True)
        returned = returned.reshape(batches * C * planes, 2, MY, MZ)
        y_back = jnp.einsum(
            "aqjk,jqpy->aypk", returned, y_inverse, preferred_element_type=jnp.float32
        ).astype(jnp.bfloat16)
        spectral = jnp.dot(
            y_back.reshape(-1, 2 * MZ), z_inverse, preferred_element_type=jnp.float32
        ).reshape(batches, C, cell_count)
        local_term = jnp.einsum(
            "bcn,co->bon", hidden_state, point_weight[layer_idx], preferred_element_type=jnp.float32
        )
        hidden_state = gelu_tanh(spectral + local_term).astype(jnp.bfloat16)
    decoded = gelu_tanh(
        jnp.einsum("bcn,cd->bdn", hidden_state, dec_in, preferred_element_type=jnp.float32)
    ).astype(jnp.bfloat16)
    decoded_out = jnp.einsum("bdn,de->ben", decoded, dec_out, preferred_element_type=jnp.float32)
    pressure = decoded_out[:, 0].reshape(batches, planes, NY, NZ)
    saturation = jax.nn.sigmoid(decoded_out[:, 1]).reshape(batches, planes, NY, NZ)
    states = jnp.stack([pressure, saturation], 1)
    conduct = mobility_of(saturation, log_perm)
    return (states, darcy(pressure, conduct, well_cells, well_rates))


BF = jnp.bfloat16
F32 = jnp.float32
PAIRS = NY // 2
PITCH = PAIRS + 8
MODE_STEP = 8
ROWS = 8
LANES = 128


def np_waves(length, kept, one_sided):
    index = np.arange(kept)
    freqs = index if one_sided else np.where(index < kept // 2, index, length - kept + index)
    angles = (freqs[:, None] * np.arange(length)[None, :] % length) * (2.0 * math.pi / length)
    norm = 1.0 / math.sqrt(length)
    return np.cos(angles) * norm, np.sin(angles) * norm


def np_forward(length, kept):
    cosine, sine = np_waves(length, kept, False)
    return np.stack([np.stack([cosine.T, -sine.T], 1), np.stack([sine.T, cosine.T], 1)], 1)


def np_inverse(length, kept):
    cosine, sine = np_waves(length, kept, False)
    return np.stack([np.stack([cosine, sine], 1), np.stack([-sine, cosine], 1)], 1)


def tables_for(count):
    own = MY // count
    cosine, sine = np_waves(NZ, MZ, True)
    twice = np.where(np.arange(MZ) == 0, 1.0, 2.0)[:, None]
    z_forward = np.concatenate([cosine.T, -sine.T], 1)
    z_inverse = np.concatenate([twice * cosine, -twice * sine], 0)
    y_forward = np_forward(NY, MY).reshape(PAIRS, 2, 2, 2, count, own)
    y_inverse = np_inverse(NY, MY).reshape(count, own, 2, 2, PAIRS, 2)
    pair = np.eye(2)
    tables = {
        "zf": np.kron(pair, z_forward),
        "zi": np.kron(pair, z_inverse),
        "yf": y_forward.transpose(3, 5, 4, 1, 2, 0).reshape(2 * MY, 2 * NY),
        "yi": y_inverse.transpose(5, 3, 4, 2, 1, 0).reshape(2 * NY, 2 * MY),
        "xf": np_forward(NX, MX).transpose(1, 2, 3, 0).reshape(2, 2 * MX, NX),
        "xi": np_inverse(NX, MX).transpose(2, 3, 0, 1).reshape(2, NX, 2 * MX),
    }
    return {name: jnp.asarray(table.astype(np.float32)).astype(BF) for name, table in tables.items()}


def dot32(a, b):
    return jnp.dot(a, b, preferred_element_type=F32)


def gelu_fast(values):
    v = values.astype(BF)
    scale = math.sqrt(2.0 / math.pi)
    inner = v * (BF(scale) + BF(scale * 0.044715) * (v * v))
    half = BF(0.5) * v
    return half + half * jnp.tanh(inner)


def swap_blocks(four):
    shape = four[0].shape
    lane = lax.broadcasted_iota(jnp.int32, shape, 1)
    low = lane < 64
    even = lane % 64 < 32
    a0, a1, a2, a3 = four

    def cross(a, b, keep, shift):
        return (
            jnp.where(keep, a, pltpu.roll(b, shift, 1)),
            jnp.where(keep, pltpu.roll(a, LANES - shift, 1), b),
        )

    b0, b2 = cross(a0, a2, low, 64)
    b1, b3 = cross(a1, a3, low, 64)
    c0, c1 = cross(b0, b1, even, 32)
    c2, c3 = cross(b2, b3, even, 32)
    return c0, c1, c2, c3


def to_modes(plane, planes, count, yf_ref, zs, send, out_ref):
    pieces = []
    for group in range(C // 4):
        four = [zs[(group * 4 + r) * PITCH : (group * 4 + r) * PITCH + PAIRS, :] for r in range(4)]
        pieces.append(jnp.concatenate([p.astype(BF) for p in swap_blocks(four)], 0))
    stacked = jnp.concatenate(pieces, 1)
    modes = dot32(yf_ref[...], stacked)
    tiles = C * MZ // LANES
    for s in range(2 * MY // count):
        for t in range(tiles):
            send[s * tiles + t, pl.ds(plane, count, stride=planes), :] = modes[
                s * count : (s + 1) * count, t * LANES : (t + 1) * LANES
            ]

    @pl.when(plane == planes - 1)
    def _():
        for t in range(send.shape[0]):
            out_ref[:, t * LANES : (t + 1) * LANES] = send[t].astype(BF)


def lay_out(zs, start, values):
    for r in range(ROWS):
        zs[pl.ds(start + r, C, stride=PITCH), :] = values[r * C : (r + 1) * C, :]


def lift_kernel(
    planes, count, feat_ref, perm_ref, in_ref, lo_ref, zf_ref, yf_ref, hid_ref, out_ref, plain, xs, zs, send
):
    plane = pl.program_id(0)

    @pl.when(plane == 0)
    def _():
        xs[...] = jnp.zeros_like(xs)

    for f in range(FIN + 1):
        plain[...] = perm_ref[0, 0] if f == FIN else feat_ref[0, f, 0].astype(F32)
        for y2 in range(2):
            xs[y2, pl.ds(f, PAIRS, stride=8), :] = plain[pl.ds(y2, PAIRS, stride=2), :]
    width = lo_ref.shape[1]

    def block(index, carry):
        start = pl.multiple_of(index * ROWS * 8, ROWS * 8)
        x = jnp.concatenate([xs[0, pl.ds(start, ROWS * 8), :], xs[1, pl.ds(start, ROWS * 8), :]], 1)
        lifted = gelu_fast(dot32(in_ref[...], x.astype(BF)))
        parts = [
            dot32(lo_ref[...], lifted[r * width : (r + 1) * width, :]).astype(BF)
            for r in range(lifted.shape[0] // width)
        ]
        hidden = jnp.concatenate(parts, 0)
        hid_ref[0, pl.ds(pl.multiple_of(index * ROWS * C, ROWS * C), ROWS * C), :] = hidden
        lay_out(zs, index * ROWS, dot32(hidden, zf_ref[...]))
        return carry

    lax.fori_loop(0, PAIRS // ROWS, block, 0)
    to_modes(plane, planes, count, yf_ref, zs, send, out_ref)


def from_modes(plane, planes, count, got_ref, yi_ref, recv, zs):
    @pl.when(plane == 0)
    def _():
        for t in range(recv.shape[0]):
            recv[t] = got_ref[:, t * LANES : (t + 1) * LANES].astype(F32)

    tiles = C * MZ // LANES
    rows = []
    for s in range(2 * MY // count):
        rows.append(
            jnp.concatenate(
                [recv[s * tiles + t, pl.ds(plane, count, stride=planes), :] for t in range(tiles)], 1
            ).astype(BF)
        )
    back = dot32(yi_ref[...], jnp.concatenate(rows, 0))
    for group in range(C // 4):
        lanes = slice(group * LANES, (group + 1) * LANES)
        four = [back[g * PAIRS : (g + 1) * PAIRS, lanes] for g in range(4)]
        for r, piece in enumerate(swap_blocks(four)):
            zs[(group * 4 + r) * PITCH : (group * 4 + r) * PITCH + PAIRS, :] = piece


def layer_rows(index, zs, hid_ref, zi_ref, kp_ref):
    start = index * ROWS
    parts = [zs[pl.ds(start + r, C, stride=PITCH), :].astype(BF) for r in range(ROWS)]
    spectral = dot32(jnp.concatenate(parts, 0), zi_ref[...])
    old = hid_ref[0, pl.ds(pl.multiple_of(index * ROWS * C, ROWS * C), ROWS * C), :]
    return gelu_fast(spectral + dot32(kp_ref[...], old))


def middle_kernel(
    planes, count, got_ref, hid_ref, kp_ref, yi_ref, zi_ref, zf_ref, yf_ref, new_ref, out_ref, recv, zs, zs2, send
):
    plane = pl.program_id(0)
    from_modes(plane, planes, count, got_ref, yi_ref, recv, zs)

    def block(index, carry):
        hidden = layer_rows(index, zs, hid_ref, zi_ref, kp_ref)
        new_ref[0, pl.ds(pl.multiple_of(index * ROWS * C, ROWS * C), ROWS * C), :] = hidden
        lay_out(zs2, index * ROWS, dot32(hidden, zf_ref[...]))
        return carry

    lax.fori_loop(0, PAIRS // ROWS, block, 0)
    to_modes(plane, planes, count, yf_ref, zs2, send, out_ref)


def final_kernel(
    planes, count, got_ref, hid_ref, kp_ref, yi_ref, zi_ref, di_ref, do_ref, perm_ref, st_ref, cond_ref, recv, zs
):
    plane = pl.program_id(0)
    from_modes(plane, planes, count, got_ref, yi_ref, recv, zs)

    def block(index, carry):
        hidden = layer_rows(index, zs, hid_ref, zi_ref, kp_ref)
        decoded = gelu_fast(dot32(di_ref[...], hidden))
        both = dot32(do_ref[...], decoded)
        for y2 in range(2):
            lanes = slice(y2 * NZ, (y2 + 1) * NZ)
            where = pl.ds(index * ROWS * 2 + y2, ROWS, stride=2)
            st_ref[0, 0, 0, where, :] = both[:ROWS, lanes]
            st_ref[0, 1, 0, where, :] = both[ROWS:, lanes]
        return carry

    lax.fori_loop(0, PAIRS // ROWS, block, 0)
    sat = jax.nn.sigmoid(st_ref[0, 1, 0])
    st_ref[0, 1, 0] = sat
    cond_ref[0, 0] = mobility_of(sat, perm_ref[0, 0])


def mix_kernel(own, a_ref, w_ref, xf_ref, xi_ref, out_ref, spec, mixed, turned, rhs):
    step = pl.program_id(0)
    half = C * own * MZ
    wide = MX * 2 * C

    @pl.when(step == 0)
    def _():
        total = dot32(xf_ref[0], a_ref[:, :half]) + dot32(xf_ref[1], a_ref[:, half:])
        spec[:, : 2 * MX] = total.T

    first = step * MODE_STEP
    base = first // MZ * (C * MZ) + first % MZ
    rows = [spec[pl.ds(base + r, C, stride=MZ), :] for r in range(MODE_STEP)]
    values = jnp.concatenate(rows, 0)[:, : 2 * MX].astype(BF)
    chunk = 512
    for piece in range(wide // chunk):
        lo = piece * chunk
        row = lax.broadcasted_iota(jnp.int32, (2 * MX, chunk), 0)
        col = lax.broadcasted_iota(jnp.int32, (2 * MX, chunk), 1) + lo
        weights = w_ref[0, :, :, lo : lo + chunk].reshape(MODE_STEP * C, chunk).astype(F32)
        sums = []
        for q in range(2):
            pick = jnp.where(row == col // (2 * C) + q * MX, 1.0, 0.0).astype(BF)
            terms = dot32(values, pick) * weights
            sums.append(jnp.sum(terms.reshape(MODE_STEP, C, chunk), 1))
        lane = lax.broadcasted_iota(jnp.int32, (MODE_STEP, chunk), 1)
        turn = jnp.where(
            lane % (2 * C) < C, -pltpu.roll(sums[1], chunk - C, 1), pltpu.roll(sums[1], C, 1)
        )
        mixed[pl.ds(pl.multiple_of(first, MODE_STEP), MODE_STEP), lo : lo + chunk] = sums[0] + turn

    @pl.when(step == pl.num_programs(0) - 1)
    def _():
        modes = own * MZ
        turned[:, :modes] = mixed[...].T
        for o in range(C):
            piece = turned[pl.ds(o, 2 * MX, stride=C), :]
            for jj in range(own):
                lo = (jj * C + o) * MZ
                rhs[:, lo : lo + MZ] = piece[:, jj * MZ : (jj + 1) * MZ]
        right = rhs[...].astype(BF)
        for p in range(2):
            out_ref[:, p * half : (p + 1) * half] = dot32(xi_ref[p], right).astype(BF)


def whole_spec(array):
    dims = array.ndim
    return pl.BlockSpec(array.shape, lambda i: (0,) * dims)


def block_diag(matrix, copies):
    rows, cols = matrix.shape
    eye = jnp.eye(copies, dtype=matrix.dtype)
    return (eye[:, None, :, None] * matrix[None, :, None, :]).reshape(copies * rows, copies * cols)


def local_fast(
    features,
    log_perm,
    well_cells,
    well_rates,
    lift_in,
    lift_out,
    spec_weight,
    point_weight,
    dec_in,
    dec_out,
):
    planes = features.shape[2]
    count = lax.axis_size("space")
    own = MY // count
    tables = tables_for(count)
    params = pltpu.CompilerParams(
        dimension_semantics=("arbitrary",), vmem_limit_bytes=56 * 1024 * 1024
    )
    sends = 2 * own * C * MZ
    tiles = sends // LANES
    hid_shape = jax.ShapeDtypeStruct((planes, PAIRS * C, 2 * NZ), BF)
    send_shape = jax.ShapeDtypeStruct((count * planes, sends), BF)
    hid_spec = pl.BlockSpec((1, PAIRS * C, 2 * NZ), lambda i: (i, 0, 0))
    send_spec = pl.BlockSpec((count * planes, sends), lambda i: (0, 0))
    zs_scratch = pltpu.VMEM((C * PITCH, LANES), F32)
    send_scratch = pltpu.VMEM((tiles, count * planes, LANES), F32)
    perm_spec = pl.BlockSpec((1, 1, NY, NZ), lambda i: (0, i, 0, 0))
    in_rows = jnp.pad(lift_in, ((0, 8 - FIN - 1), (0, 0))).T
    k_in = block_diag(in_rows, ROWS)
    k_lo = block_diag(lift_out.T, 2)
    k_di = block_diag(dec_in.T, ROWS)
    eye = jnp.eye(ROWS, dtype=BF)
    k_do = (dec_out.T[:, None, None, :] * eye[None, :, :, None]).reshape(2 * ROWS, -1)

    def swap(sent):
        return lax.all_to_all(
            sent.reshape(count, planes, sends), "space", split_axis=0, concat_axis=0, tiled=True
        ).reshape(count * planes, sends)

    operands = (features, log_perm, k_in, k_lo, tables["zf"], tables["yf"])
    hidden, sent = pl.pallas_call(
        lambda *refs: lift_kernel(planes, count, *refs),
        grid=(planes,),
        in_specs=[pl.BlockSpec((1, FIN, 1, NY, NZ), lambda i: (0, 0, i, 0, 0)), perm_spec]
        + [whole_spec(a) for a in operands[2:]],
        out_specs=[hid_spec, send_spec],
        out_shape=[hid_shape, send_shape],
        scratch_shapes=[
            pltpu.VMEM((NY, NZ), F32),
            pltpu.VMEM((2, PAIRS * 8, NZ), F32),
            zs_scratch,
            send_scratch,
        ],
        compiler_params=params,
        name="lift",
    )(*operands)
    for layer_idx in range(LAYERS):
        arrived = swap(sent)
        modes = own * MZ
        mixed = pl.pallas_call(
            lambda *refs: mix_kernel(own, *refs),
            grid=(modes // MODE_STEP,),
            in_specs=[
                send_spec,
                pl.BlockSpec(
                    (1, MODE_STEP, C, MX * 2 * C), lambda i, layer=layer_idx: (layer, i, 0, 0)
                ),
                whole_spec(tables["xf"]),
                whole_spec(tables["xi"]),
            ],
            out_specs=send_spec,
            out_shape=send_shape,
            scratch_shapes=[
                pltpu.VMEM((modes * C, LANES), F32),
                pltpu.VMEM((modes, MX * 2 * C), F32),
                pltpu.VMEM((MX * 2 * C, LANES), F32),
                pltpu.VMEM((2 * MX, modes * C), F32),
            ],
            compiler_params=params,
            name="mix",
        )(arrived, spec_weight, tables["xf"], tables["xi"])
        returned = swap(mixed)
        k_p = block_diag(point_weight[layer_idx].T, ROWS)
        shared = (returned, hidden, k_p, tables["yi"], tables["zi"])
        shared_specs = [send_spec, hid_spec] + [whole_spec(a) for a in shared[2:]]
        if layer_idx < LAYERS - 1:
            operands = shared + (tables["zf"], tables["yf"])
            hidden, sent = pl.pallas_call(
                lambda *refs: middle_kernel(planes, count, *refs),
                grid=(planes,),
                in_specs=shared_specs + [whole_spec(a) for a in operands[5:]],
                out_specs=[hid_spec, send_spec],
                out_shape=[hid_shape, send_shape],
                scratch_shapes=[send_scratch, zs_scratch, zs_scratch, send_scratch],
                compiler_params=params,
                name="middle",
            )(*operands)
        else:
            states, conduct = pl.pallas_call(
                lambda *refs: final_kernel(planes, count, *refs),
                grid=(planes,),
                in_specs=shared_specs + [whole_spec(k_di), whole_spec(k_do), perm_spec],
                out_specs=[pl.BlockSpec((1, 2, 1, NY, NZ), lambda i: (0, 0, i, 0, 0)), perm_spec],
                out_shape=[
                    jax.ShapeDtypeStruct((1, 2, planes, NY, NZ), F32),
                    jax.ShapeDtypeStruct((1, planes, NY, NZ), F32),
                ],
                scratch_shapes=[send_scratch, zs_scratch],
                compiler_params=params,
                name="final",
            )(*shared, k_di, k_do, log_perm)
    return (states, darcy(states[:, 0], conduct, well_cells, well_rates))


def local(features, log_perm, well_cells, well_rates, lift_in, lift_out, spec_weight, *rest):
    batches, planes = features.shape[0], features.shape[2]
    count = lax.axis_size("space")
    fits = batches == 1 and planes == 8 and count % 8 == 0 and MY % count == 0
    run = local_fast if fits else local_general
    return run(
        features, log_perm, well_cells, well_rates, lift_in, lift_out, spec_weight, *rest
    )


def solution(mesh):
    return jax.shard_map(
        local,
        mesh=mesh,
        in_specs=(
            P("sample", None, "space", None, None),
            P("sample", "space", None, None),
            P("sample", None),
            P("sample", None),
            P(),
            P(),
            P(None, "space", None, None),
            P(),
            P(),
            P(),
        ),
        out_specs=(P("sample", None, "space", None, None), P("sample", "space", None, None)),
        check_vma=False,
    )
```

```python
import math

import jax
import jax.numpy as jnp
import numpy as np
from jax import lax
from jax.experimental import pallas as pl
from jax.experimental.pallas import tpu as pltpu
from jax.sharding import PartitionSpec as P

NX = 128
NY = 128
NZ = 128
MX = 32
MY = 32
MZ = 32
C = 32
FIN = 4
LAYERS = 2
WELLS = 32


def padded_2(block, sides, width):
    for axis, dim in sides:
        count = lax.axis_size(axis)
        forward = [(i, i + 1) for i in range(count - 1)]
        backward = [(target, source) for source, target in forward]
        low = lax.ppermute(
            lax.slice_in_dim(block, block.shape[dim] - width, None, axis=dim), axis, forward
        )
        high = lax.ppermute(lax.slice_in_dim(block, 0, width, axis=dim), axis, backward)
        block = jnp.concatenate([low, block, high], axis=dim)
    return block


def freq_table(length, kept, one_sided):
    indices = jnp.arange(kept, dtype=jnp.int32)
    if one_sided:
        return indices
    return jnp.where(indices < kept // 2, indices, length - kept + indices)


def wave_parts(length, kept, one_sided):
    freqs = freq_table(length, kept, one_sided)
    places = jnp.arange(length, dtype=jnp.int32)
    phase_turns = freqs[:, None] * places[None, :] % length
    angles = phase_turns.astype(jnp.float32) * (2.0 * math.pi / length)
    norm_scale = 1.0 / math.sqrt(length)
    return (jnp.cos(angles) * norm_scale, jnp.sin(angles) * norm_scale)


def forward_table(length, kept):
    cosine_vals, sine_vals = wave_parts(length, kept, False)
    return jnp.stack(
        [jnp.stack([cosine_vals.T, -sine_vals.T], 1), jnp.stack([sine_vals.T, cosine_vals.T], 1)], 1
    ).astype(jnp.bfloat16)


def inverse_table(length, kept):
    cosine_vals, sine_vals = wave_parts(length, kept, False)
    return jnp.stack(
        [jnp.stack([cosine_vals, sine_vals], 1), jnp.stack([-sine_vals, cosine_vals], 1)], 1
    ).astype(jnp.bfloat16)


def z_tables():
    cosine_vals, sine_vals = wave_parts(NZ, MZ, True)
    weights_k = jnp.where(jnp.arange(MZ) == 0, 1.0, 2.0).astype(jnp.float32)[:, None]
    z_forward = jnp.concatenate([cosine_vals.T, -sine_vals.T], 1).astype(jnp.bfloat16)
    z_inverse = jnp.concatenate([weights_k * cosine_vals, -weights_k * sine_vals], 0).astype(
        jnp.bfloat16
    )
    return (z_forward, z_inverse)


def gelu_tanh(values):
    return jax.nn.gelu(values, approximate=True)


def face_term(cond_a, cond_b, press_a, press_b):
    return 2.0 * cond_a * cond_b / (cond_a + cond_b) * (press_a - press_b)


def mobility_of(saturation, log_values):
    return jnp.exp(log_values) * (
        saturation * saturation + 0.5 * (1.0 - saturation) * (1.0 - saturation)
    )


def darcy(pressure, conduct, well_cells, well_rates):
    batches, planes = pressure.shape[0], pressure.shape[1]
    space_index = lax.axis_index("space")
    pad_cond = jnp.pad(conduct, ((0, 0), (0, 0), (1, 1), (1, 1)))
    pad_press = jnp.pad(pressure, ((0, 0), (0, 0), (1, 1), (1, 1)))
    flux_sum = face_term(conduct, pad_cond[:, :, 2:, 1:-1], pressure, pad_press[:, :, 2:, 1:-1])
    flux_sum = flux_sum + face_term(
        conduct, pad_cond[:, :, :-2, 1:-1], pressure, pad_press[:, :, :-2, 1:-1]
    )
    flux_sum = flux_sum + face_term(
        conduct, pad_cond[:, :, 1:-1, 2:], pressure, pad_press[:, :, 1:-1, 2:]
    )
    flux_sum = flux_sum + face_term(
        conduct, pad_cond[:, :, 1:-1, :-2], pressure, pad_press[:, :, 1:-1, :-2]
    )
    fields = jnp.stack([pressure, conduct], 1)
    padded = padded_2(fields.astype(jnp.bfloat16), (("space", 2),), 1).astype(fields.dtype)
    press_low = padded[:, 0, 0]
    press_high = padded[:, 0, -1]
    cond_low = padded[:, 1, 0]
    cond_high = padded[:, 1, -1]
    press_below = jnp.concatenate([press_low[:, None], pressure[:, :-1]], 1)
    cond_below = jnp.concatenate([cond_low[:, None], conduct[:, :-1]], 1)
    press_above = jnp.concatenate([pressure[:, 1:], press_high[:, None]], 1)
    cond_above = jnp.concatenate([conduct[:, 1:], cond_high[:, None]], 1)
    lower_terms = face_term(conduct, cond_below, pressure, press_below)
    upper_terms = face_term(conduct, cond_above, pressure, press_above)
    flux_sum = flux_sum + lower_terms + upper_terms
    well_x = well_cells // (NY * NZ) - space_index * planes
    well_y = well_cells // NZ % NY
    well_z = well_cells % NZ
    onehot_x = (well_x[:, :, None] == jnp.arange(planes, dtype=jnp.int32)[None, None, :]).astype(
        jnp.float32
    ) * well_rates[:, :, None]
    onehot_y = (well_y[:, :, None] == jnp.arange(NY, dtype=jnp.int32)[None, None, :]).astype(
        jnp.float32
    )
    onehot_z = (well_z[:, :, None] == jnp.arange(NZ, dtype=jnp.int32)[None, None, :]).astype(
        jnp.float32
    )
    plane_rows = (onehot_x[:, :, :, None] * onehot_y[:, :, None, :]).reshape(
        batches, WELLS, planes * NY
    )
    source = jnp.einsum(
        "bwa,bwz->baz", plane_rows, onehot_z, precision=lax.Precision.HIGHEST
    ).reshape(batches, planes, NY, NZ)
    return flux_sum - source


def local_general(
    features,
    log_perm,
    well_cells,
    well_rates,
    lift_in,
    lift_out,
    spec_weight,
    point_weight,
    dec_in,
    dec_out,
):
    batches = features.shape[0]
    planes = features.shape[2]
    space_index = lax.axis_index("space")
    block = spec_weight.shape[1]
    cell_count = planes * NY * NZ
    z_forward, z_inverse = z_tables()
    y_forward = forward_table(NY, MY)
    y_inverse = inverse_table(NY, MY)
    x_forward = forward_table(NX, MX)
    x_inverse = inverse_table(NX, MX)
    perm_b = log_perm.astype(jnp.bfloat16).reshape(batches, 1, cell_count)
    lift_input = jnp.concatenate([features.reshape(batches, FIN, cell_count), perm_b], 1)
    lift_hidden = jnp.einsum("bfn,fh->bhn", lift_input, lift_in, preferred_element_type=jnp.float32)
    lifted = gelu_tanh(lift_hidden).astype(jnp.bfloat16)
    hidden_state = jnp.einsum(
        "bhn,hc->bcn", lifted, lift_out, preferred_element_type=jnp.float32
    ).astype(jnp.bfloat16)
    for layer_idx in range(LAYERS):
        zspec = jnp.dot(hidden_state.reshape(-1, NZ), z_forward, preferred_element_type=jnp.float32)
        zspec = zspec.astype(jnp.bfloat16).reshape(batches * C * planes, NY, 2, MZ)
        yz_spec = jnp.einsum(
            "aypk,ypqj->aqjk", zspec, y_forward, preferred_element_type=jnp.float32
        )
        yz_spec = yz_spec.astype(jnp.bfloat16).reshape(batches, C, planes, 2, MY * MZ)
        mode_weights = spec_weight[layer_idx].reshape(block, C, MX, 2, C)
        spectrum = jnp.einsum(
            "bcxpm,xpqi->bcqim",
            lax.all_to_all(yz_spec, "space", split_axis=4, concat_axis=2, tiled=True),
            x_forward,
            preferred_element_type=jnp.float32,
        ).astype(jnp.bfloat16)
        products = jnp.einsum(
            "bcqim,mcipo->bimqpo", spectrum, mode_weights, preferred_element_type=jnp.float32
        )
        real_part = products[:, :, :, 0, 0] - products[:, :, :, 1, 1]
        imag_part = products[:, :, :, 0, 1] + products[:, :, :, 1, 0]
        mixed_modes = jnp.stack([real_part, imag_part], 3).astype(jnp.bfloat16)
        back_field = jnp.einsum(
            "bimqo,iqpx->boxpm", mixed_modes, x_inverse, preferred_element_type=jnp.float32
        ).astype(jnp.bfloat16)
        returned = lax.all_to_all(back_field, "space", split_axis=2, concat_axis=4, tiled=True)
        returned = returned.reshape(batches * C * planes, 2, MY, MZ)
        y_back = jnp.einsum(
            "aqjk,jqpy->aypk", returned, y_inverse, preferred_element_type=jnp.float32
        ).astype(jnp.bfloat16)
        spectral = jnp.dot(
            y_back.reshape(-1, 2 * MZ), z_inverse, preferred_element_type=jnp.float32
        ).reshape(batches, C, cell_count)
        local_term = jnp.einsum(
            "bcn,co->bon", hidden_state, point_weight[layer_idx], preferred_element_type=jnp.float32
        )
        hidden_state = gelu_tanh(spectral + local_term).astype(jnp.bfloat16)
    decoded = gelu_tanh(
        jnp.einsum("bcn,cd->bdn", hidden_state, dec_in, preferred_element_type=jnp.float32)
    ).astype(jnp.bfloat16)
    decoded_out = jnp.einsum("bdn,de->ben", decoded, dec_out, preferred_element_type=jnp.float32)
    pressure = decoded_out[:, 0].reshape(batches, planes, NY, NZ)
    saturation = jax.nn.sigmoid(decoded_out[:, 1]).reshape(batches, planes, NY, NZ)
    states = jnp.stack([pressure, saturation], 1)
    conduct = mobility_of(saturation, log_perm)
    return (states, darcy(pressure, conduct, well_cells, well_rates))


BF = jnp.bfloat16
F32 = jnp.float32
PAIRS = NY // 2
PITCH = PAIRS + 8
MODE_STEP = 8
ROWS = 8
LANES = 128


def np_waves(length, kept, one_sided):
    index = np.arange(kept)
    freqs = index if one_sided else np.where(index < kept // 2, index, length - kept + index)
    angles = (freqs[:, None] * np.arange(length)[None, :] % length) * (2.0 * math.pi / length)
    norm = 1.0 / math.sqrt(length)
    return np.cos(angles) * norm, np.sin(angles) * norm


def np_forward(length, kept):
    cosine, sine = np_waves(length, kept, False)
    return np.stack([np.stack([cosine.T, -sine.T], 1), np.stack([sine.T, cosine.T], 1)], 1)


def np_inverse(length, kept):
    cosine, sine = np_waves(length, kept, False)
    return np.stack([np.stack([cosine, sine], 1), np.stack([-sine, cosine], 1)], 1)


def by_plane(table, axis, count):
    planes = NX // count
    order = np.arange(NX).reshape(count, planes).T.reshape(-1)
    return np.take(table, order, axis)


def tables_for(count):
    own = MY // count
    cosine, sine = np_waves(NZ, MZ, True)
    twice = np.where(np.arange(MZ) == 0, 1.0, 2.0)[:, None]
    z_forward = np.concatenate([cosine.T, -sine.T], 1)
    z_inverse = np.concatenate([twice * cosine, -twice * sine], 0)
    y_forward = np_forward(NY, MY).reshape(PAIRS, 2, 2, 2, count, own)
    y_inverse = np_inverse(NY, MY).reshape(count, own, 2, 2, PAIRS, 2)
    pair = np.eye(2)
    tables = {
        "zf": np.kron(pair, z_forward),
        "zi": np.kron(pair, z_inverse),
        "yf": y_forward.transpose(3, 5, 4, 1, 2, 0).reshape(2 * MY, 2 * NY),
        "yi": y_inverse.transpose(5, 3, 4, 2, 1, 0).reshape(2 * NY, 2 * MY),
        "xf": by_plane(np_forward(NX, MX).transpose(1, 2, 3, 0).reshape(2, 2 * MX, NX), 2, count),
        "xi": by_plane(np_inverse(NX, MX).transpose(2, 3, 0, 1).reshape(2, NX, 2 * MX), 1, count),
    }
    return {name: jnp.asarray(table.astype(np.float32)).astype(BF) for name, table in tables.items()}


def dot32(a, b):
    return jnp.dot(a, b, preferred_element_type=F32)


def gelu_fast(values):
    v = values.astype(BF)
    scale = math.sqrt(2.0 / math.pi)
    inner = v * (BF(scale) + BF(scale * 0.044715) * (v * v))
    half = BF(0.5) * v
    return half + half * jnp.tanh(inner)


def swap_blocks(four):
    shape = four[0].shape
    lane = lax.broadcasted_iota(jnp.int32, shape, 1)
    low = lane < 64
    even = lane % 64 < 32
    a0, a1, a2, a3 = four

    def cross(a, b, keep, shift):
        return (
            jnp.where(keep, a, pltpu.roll(b, shift, 1)),
            jnp.where(keep, pltpu.roll(a, LANES - shift, 1), b),
        )

    b0, b2 = cross(a0, a2, low, 64)
    b1, b3 = cross(a1, a3, low, 64)
    c0, c1 = cross(b0, b1, even, 32)
    c2, c3 = cross(b2, b3, even, 32)
    return c0, c1, c2, c3


def send_plane(me, count, plane, send, recv, send_sem, recv_sem):
    for shift in range(1, count):
        target = lax.rem(me + shift, count)
        pltpu.make_async_remote_copy(
            src_ref=send.at[plane, target],
            dst_ref=recv.at[plane, me],
            send_sem=send_sem.at[plane],
            recv_sem=recv_sem.at[plane],
            device_id={"space": target},
            device_id_type=pl.DeviceIdType.MESH,
        ).start()
    recv[plane, me] = send[plane, me]


def wait_plane(count, plane, buffer, sem):
    part = buffer.at[plane, pl.ds(0, count - 1)]
    pltpu.make_async_copy(part, part, sem.at[plane]).wait()


def to_modes(plane, count, yf_ref, zs, flat, send):
    pieces = []
    for group in range(C // 4):
        four = [zs[(group * 4 + r) * PITCH : (group * 4 + r) * PITCH + PAIRS, :] for r in range(4)]
        pieces.append(jnp.concatenate([p.astype(BF) for p in swap_blocks(four)], 0))
    modes = dot32(yf_ref[...], jnp.concatenate(pieces, 1))
    tiles = C * MZ // LANES
    slots = 2 * MY // count * tiles
    for s in range(2 * MY // count):
        for t in range(tiles):
            flat[pl.ds(s * tiles + t, count, stride=slots), :] = modes[
                s * count : (s + 1) * count, t * LANES : (t + 1) * LANES
            ]
    send[plane] = flat[: count * slots, :].reshape(count, slots, LANES).astype(BF)


def lay_out(zs, start, values):
    for r in range(ROWS):
        zs[pl.ds(start + r, C, stride=PITCH), :] = values[r * C : (r + 1) * C, :]


def hid_rows(index):
    return pl.ds(pl.multiple_of(index * ROWS * C, ROWS * C), ROWS * C)


def lift_plane(plane, feat_ref, perm_ref, in_ref, lo_ref, zf_ref, hid, plain, xs, zs):
    for f in range(FIN + 1):
        plain[...] = perm_ref[0, plane] if f == FIN else feat_ref[0, f, plane].astype(F32)
        for y2 in range(2):
            xs[y2, pl.ds(f, PAIRS, stride=8), :] = plain[pl.ds(y2, PAIRS, stride=2), :]
    width = lo_ref.shape[1]

    def block(index, carry):
        start = pl.multiple_of(index * ROWS * 8, ROWS * 8)
        x = jnp.concatenate([xs[0, pl.ds(start, ROWS * 8), :], xs[1, pl.ds(start, ROWS * 8), :]], 1)
        lifted = gelu_fast(dot32(in_ref[...], x.astype(BF)))
        parts = [
            dot32(lo_ref[...], lifted[r * width : (r + 1) * width, :]).astype(BF)
            for r in range(lifted.shape[0] // width)
        ]
        hidden = jnp.concatenate(parts, 0)
        hid[plane, hid_rows(index), :] = hidden
        lay_out(zs, index * ROWS, dot32(hidden, zf_ref[...]))
        return carry

    lax.fori_loop(0, PAIRS // ROWS, block, 0)


def from_modes(plane, count, recv, yi_ref, flat, zs):
    tiles = C * MZ // LANES
    slots = 2 * MY // count * tiles
    flat[: count * slots, :] = recv[plane].astype(F32).reshape(count * slots, LANES)
    rows = []
    for s in range(2 * MY // count):
        rows.append(
            jnp.concatenate(
                [flat[pl.ds(s * tiles + t, count, stride=slots), :] for t in range(tiles)], 1
            ).astype(BF)
        )
    back = dot32(yi_ref[...], jnp.concatenate(rows, 0))
    for group in range(C // 4):
        lanes = slice(group * LANES, (group + 1) * LANES)
        four = [back[g * PAIRS : (g + 1) * PAIRS, lanes] for g in range(4)]
        for r, piece in enumerate(swap_blocks(four)):
            zs[(group * 4 + r) * PITCH : (group * 4 + r) * PITCH + PAIRS, :] = piece


def layer_rows(plane, index, zs, hid, zi_ref, kp):
    start = index * ROWS
    parts = [zs[pl.ds(start + r, C, stride=PITCH), :].astype(BF) for r in range(ROWS)]
    spectral = dot32(jnp.concatenate(parts, 0), zi_ref[...])
    return gelu_fast(spectral + dot32(kp, hid[plane, hid_rows(index), :]))


def middle_plane(plane, kp, zi_ref, zf_ref, hid, zs, zs2):
    def block(index, carry):
        hidden = layer_rows(plane, index, zs, hid, zi_ref, kp)
        hid[plane, hid_rows(index), :] = hidden
        lay_out(zs2, index * ROWS, dot32(hidden, zf_ref[...]))
        return carry

    lax.fori_loop(0, PAIRS // ROWS, block, 0)


def final_plane(plane, kp, zi_ref, di_ref, do_ref, perm_ref, hid, zs, st_ref, cond_ref):
    def block(index, carry):
        hidden = layer_rows(plane, index, zs, hid, zi_ref, kp)
        both = dot32(do_ref[...], gelu_fast(dot32(di_ref[...], hidden)))
        for y2 in range(2):
            lanes = slice(y2 * NZ, (y2 + 1) * NZ)
            where = pl.ds(index * ROWS * 2 + y2, ROWS, stride=2)
            st_ref[0, 0, plane, where, :] = both[:ROWS, lanes]
            st_ref[0, 1, plane, where, :] = both[ROWS:, lanes]
        return carry

    lax.fori_loop(0, PAIRS // ROWS, block, 0)
    sat = jax.nn.sigmoid(st_ref[0, 1, plane])
    st_ref[0, 1, plane] = sat
    cond_ref[0, plane] = mobility_of(sat, perm_ref[0, plane])


def mix_modes(planes, count, recv, send, wbuf, xf_ref, xi_ref, flat, spec, mixed, turned, rhs):
    own = MY // count
    tiles = C * MZ // LANES
    slots = 2 * own * tiles
    every = count * planes
    wide = MX * 2 * C
    for plane in range(planes):
        flat[plane * count * slots : (plane + 1) * count * slots, :] = (
            recv[plane].astype(F32).reshape(count * slots, LANES)
        )
    total = 0.0
    for p in range(2):
        right = jnp.concatenate(
            [
                flat[pl.ds(p * own * tiles + t, every, stride=slots), :].astype(BF)
                for t in range(own * tiles)
            ],
            1,
        )
        total = total + dot32(xf_ref[p], right)
    spec[:, : 2 * MX] = total.T
    chunk = 512

    def step(index, carry):
        first = pl.multiple_of(index * MODE_STEP, MODE_STEP)
        base = first // MZ * (C * MZ) + first % MZ
        rows = [spec[pl.ds(base + r, C, stride=MZ), :] for r in range(MODE_STEP)]
        values = jnp.concatenate(rows, 0)[:, : 2 * MX].astype(BF)
        for piece in range(wide // chunk):
            lo = piece * chunk
            row = lax.broadcasted_iota(jnp.int32, (2 * MX, chunk), 0)
            col = lax.broadcasted_iota(jnp.int32, (2 * MX, chunk), 1) + lo
            weights = wbuf[pl.ds(first, MODE_STEP), :, lo : lo + chunk]
            weights = weights.reshape(MODE_STEP * C, chunk).astype(F32)
            sums = []
            for q in range(2):
                pick = jnp.where(row == col // (2 * C) + q * MX, 1.0, 0.0).astype(BF)
                terms = dot32(values, pick) * weights
                sums.append(jnp.sum(terms.reshape(MODE_STEP, C, chunk), 1))
            lane = lax.broadcasted_iota(jnp.int32, (MODE_STEP, chunk), 1)
            turn = jnp.where(
                lane % (2 * C) < C, -pltpu.roll(sums[1], chunk - C, 1), pltpu.roll(sums[1], C, 1)
            )
            mixed[pl.ds(first, MODE_STEP), lo : lo + chunk] = sums[0] + turn
        return carry

    lax.fori_loop(0, own * MZ // MODE_STEP, step, 0)
    turned[:, : own * MZ] = mixed[...].T
    for o in range(C):
        piece = turned[pl.ds(o, 2 * MX, stride=C), :]
        for jj in range(own):
            lo = (jj * C + o) * MZ
            rhs[:, lo : lo + MZ] = piece[:, jj * MZ : (jj + 1) * MZ]
    right = rhs[...].astype(BF)
    for p in range(2):
        back = dot32(xi_ref[p], right)
        for t in range(own * tiles):
            flat[pl.ds(p * own * tiles + t, every, stride=slots), :] = back[
                :, t * LANES : (t + 1) * LANES
            ]
    for plane in range(planes):
        send[plane] = (
            flat[plane * count * slots : (plane + 1) * count * slots, :]
            .reshape(count, slots, LANES)
            .astype(BF)
        )


def whole_kernel(
    planes, count, feat_ref, perm_ref, in_ref, lo_ref, kp_ref, di_ref, do_ref, zf_ref, zi_ref,
    yf_ref, yi_ref, xf_ref, xi_ref, w_hbm, st_ref, cond_ref,
    hid, wbuf, send_f, recv_f, send_b, recv_b, flat, spec, mixed, turned, rhs, zs, zs2, xs, plain,
    w_sem, sf_sem, rf_sem, sb_sem, rb_sem,
):
    me = lax.axis_index("space")
    barrier = pltpu.get_barrier_semaphore()
    for shift in range(1, count):
        pl.semaphore_signal(
            barrier,
            inc=1,
            device_id={"space": lax.rem(me + shift, count)},
            device_id_type=pl.DeviceIdType.MESH,
        )
    fetch = pltpu.make_async_copy(w_hbm.at[0], wbuf, w_sem.at[0])
    fetch.start()
    xs[...] = jnp.zeros_like(xs)
    pl.semaphore_wait(barrier, count - 1)

    def over(body):
        def run(plane, carry):
            body(plane)
            return carry

        lax.fori_loop(0, planes, run, 0)

    def lift(plane):
        lift_plane(plane, feat_ref, perm_ref, in_ref, lo_ref, zf_ref, hid, plain, xs, zs)
        to_modes(plane, count, yf_ref, zs, flat, send_f)
        send_plane(me, count, plane, send_f, recv_f, sf_sem, rf_sem)

    over(lift)
    for layer in range(LAYERS):
        fetch.wait()
        over(lambda plane: wait_plane(count, plane, recv_f, rf_sem))
        over(lambda plane: wait_plane(count, plane, send_f, sf_sem))
        mix_modes(
            planes, count, recv_f, send_b, wbuf, xf_ref, xi_ref, flat, spec, mixed, turned, rhs
        )
        if layer + 1 < LAYERS:
            fetch = pltpu.make_async_copy(w_hbm.at[layer + 1], wbuf, w_sem.at[layer + 1])
            fetch.start()
        over(lambda plane: send_plane(me, count, plane, send_b, recv_b, sb_sem, rb_sem))

        def rest(plane):
            wait_plane(count, plane, recv_b, rb_sem)
            from_modes(plane, count, recv_b, yi_ref, flat, zs)
            if layer + 1 < LAYERS:
                middle_plane(plane, kp_ref[layer], zi_ref, zf_ref, hid, zs, zs2)
                to_modes(plane, count, yf_ref, zs2, flat, send_f)
                send_plane(me, count, plane, send_f, recv_f, sf_sem, rf_sem)
            else:
                final_plane(
                    plane, kp_ref[layer], zi_ref, di_ref, do_ref, perm_ref, hid, zs, st_ref, cond_ref
                )

        over(rest)
        over(lambda plane: wait_plane(count, plane, send_b, sb_sem))


def block_diag(matrix, copies):
    rows, cols = matrix.shape
    eye = jnp.eye(copies, dtype=matrix.dtype)
    return (eye[:, None, :, None] * matrix[None, :, None, :]).reshape(copies * rows, copies * cols)


def local_fast(
    features,
    log_perm,
    well_cells,
    well_rates,
    lift_in,
    lift_out,
    spec_weight,
    point_weight,
    dec_in,
    dec_out,
):
    planes = features.shape[2]
    count = lax.axis_size("space")
    own = MY // count
    modes = own * MZ
    slots = 2 * modes * C // LANES
    tables = tables_for(count)
    in_rows = jnp.pad(lift_in, ((0, 0 + 8 - FIN - 1), (0, 0))).T
    k_p = jnp.stack([block_diag(point_weight[layer].T, ROWS) for layer in range(LAYERS)])
    eye = jnp.eye(ROWS, dtype=BF)
    k_do = (dec_out.T[:, None, None, :] * eye[None, :, :, None]).reshape(2 * ROWS, -1)
    operands = (
        features,
        log_perm,
        block_diag(in_rows, ROWS),
        block_diag(lift_out.T, 2),
        k_p,
        block_diag(dec_in.T, ROWS),
        k_do,
    ) + tuple(tables[name] for name in ("zf", "zi", "yf", "yi", "xf", "xi"))
    vmem = pl.BlockSpec(memory_space=pltpu.VMEM)
    exchange = pltpu.VMEM((planes, count, slots, LANES), BF)
    states, conduct = pl.pallas_call(
        lambda *refs: whole_kernel(planes, count, *refs),
        in_specs=[vmem] * len(operands) + [pl.BlockSpec(memory_space=pl.ANY)],
        out_specs=[vmem, vmem],
        out_shape=[
            jax.ShapeDtypeStruct((1, 2, planes, NY, NZ), F32),
            jax.ShapeDtypeStruct((1, planes, NY, NZ), F32),
        ],
        scratch_shapes=[
            pltpu.VMEM((planes, PAIRS * C, 2 * NZ), BF),
            pltpu.VMEM(spec_weight.shape[1:], BF),
            exchange,
            exchange,
            exchange,
            exchange,
            pltpu.VMEM((planes * count * slots, LANES), F32),
            pltpu.VMEM((modes * C, LANES), F32),
            pltpu.VMEM((modes, MX * 2 * C), F32),
            pltpu.VMEM((MX * 2 * C, LANES), F32),
            pltpu.VMEM((2 * MX, modes * C), F32),
            pltpu.VMEM((C * PITCH, LANES), F32),
            pltpu.VMEM((C * PITCH, LANES), F32),
            pltpu.VMEM((2, PAIRS * 8, NZ), F32),
            pltpu.VMEM((NY, NZ), F32),
            pltpu.SemaphoreType.DMA((LAYERS,)),
        ]
        + [pltpu.SemaphoreType.DMA((planes,))] * 4,
        compiler_params=pltpu.CompilerParams(
            collective_id=0, has_side_effects=True, vmem_limit_bytes=60 * 1024 * 1024
        ),
        name="whole",
    )(*operands, spec_weight)
    return (states, darcy(states[:, 0], conduct, well_cells, well_rates))


def local(features, log_perm, well_cells, well_rates, lift_in, lift_out, spec_weight, *rest):
    batches, planes = features.shape[0], features.shape[2]
    count = lax.axis_size("space")
    fits = batches == 1 and planes == 8 and count % 8 == 0 and MY % count == 0
    run = local_fast if fits else local_general
    return run(
        features, log_perm, well_cells, well_rates, lift_in, lift_out, spec_weight, *rest
    )


def solution(mesh):
    return jax.shard_map(
        local,
        mesh=mesh,
        in_specs=(
            P("sample", None, "space", None, None),
            P("sample", "space", None, None),
            P("sample", None),
            P("sample", None),
            P(),
            P(),
            P(None, "space", None, None),
            P(),
            P(),
            P(),
        ),
        out_specs=(P("sample", None, "space", None, None), P("sample", "space", None, None)),
        check_vma=False,
    )
```

```python
import math

import jax
import jax.numpy as jnp
import numpy as np
from jax import lax
from jax.experimental import pallas as pl
from jax.experimental.pallas import tpu as pltpu
from jax.sharding import PartitionSpec as P

NX = 128
NY = 128
NZ = 128
MX = 32
MY = 32
MZ = 32
C = 32
FIN = 4
LAYERS = 2
WELLS = 32


def padded_2(block, sides, width):
    for axis, dim in sides:
        count = lax.axis_size(axis)
        forward = [(i, i + 1) for i in range(count - 1)]
        backward = [(target, source) for source, target in forward]
        low = lax.ppermute(
            lax.slice_in_dim(block, block.shape[dim] - width, None, axis=dim), axis, forward
        )
        high = lax.ppermute(lax.slice_in_dim(block, 0, width, axis=dim), axis, backward)
        block = jnp.concatenate([low, block, high], axis=dim)
    return block


def freq_table(length, kept, one_sided):
    indices = jnp.arange(kept, dtype=jnp.int32)
    if one_sided:
        return indices
    return jnp.where(indices < kept // 2, indices, length - kept + indices)


def wave_parts(length, kept, one_sided):
    freqs = freq_table(length, kept, one_sided)
    places = jnp.arange(length, dtype=jnp.int32)
    phase_turns = freqs[:, None] * places[None, :] % length
    angles = phase_turns.astype(jnp.float32) * (2.0 * math.pi / length)
    norm_scale = 1.0 / math.sqrt(length)
    return (jnp.cos(angles) * norm_scale, jnp.sin(angles) * norm_scale)


def forward_table(length, kept):
    cosine_vals, sine_vals = wave_parts(length, kept, False)
    return jnp.stack(
        [jnp.stack([cosine_vals.T, -sine_vals.T], 1), jnp.stack([sine_vals.T, cosine_vals.T], 1)], 1
    ).astype(jnp.bfloat16)


def inverse_table(length, kept):
    cosine_vals, sine_vals = wave_parts(length, kept, False)
    return jnp.stack(
        [jnp.stack([cosine_vals, sine_vals], 1), jnp.stack([-sine_vals, cosine_vals], 1)], 1
    ).astype(jnp.bfloat16)


def z_tables():
    cosine_vals, sine_vals = wave_parts(NZ, MZ, True)
    weights_k = jnp.where(jnp.arange(MZ) == 0, 1.0, 2.0).astype(jnp.float32)[:, None]
    z_forward = jnp.concatenate([cosine_vals.T, -sine_vals.T], 1).astype(jnp.bfloat16)
    z_inverse = jnp.concatenate([weights_k * cosine_vals, -weights_k * sine_vals], 0).astype(
        jnp.bfloat16
    )
    return (z_forward, z_inverse)


def gelu_tanh(values):
    return jax.nn.gelu(values, approximate=True)


def face_term(cond_a, cond_b, press_a, press_b):
    return 2.0 * cond_a * cond_b / (cond_a + cond_b) * (press_a - press_b)


def mobility_of(saturation, log_values):
    return jnp.exp(log_values) * (
        saturation * saturation + 0.5 * (1.0 - saturation) * (1.0 - saturation)
    )


def darcy(pressure, conduct, well_cells, well_rates):
    batches, planes = pressure.shape[0], pressure.shape[1]
    space_index = lax.axis_index("space")
    pad_cond = jnp.pad(conduct, ((0, 0), (0, 0), (1, 1), (1, 1)))
    pad_press = jnp.pad(pressure, ((0, 0), (0, 0), (1, 1), (1, 1)))
    flux_sum = face_term(conduct, pad_cond[:, :, 2:, 1:-1], pressure, pad_press[:, :, 2:, 1:-1])
    flux_sum = flux_sum + face_term(
        conduct, pad_cond[:, :, :-2, 1:-1], pressure, pad_press[:, :, :-2, 1:-1]
    )
    flux_sum = flux_sum + face_term(
        conduct, pad_cond[:, :, 1:-1, 2:], pressure, pad_press[:, :, 1:-1, 2:]
    )
    flux_sum = flux_sum + face_term(
        conduct, pad_cond[:, :, 1:-1, :-2], pressure, pad_press[:, :, 1:-1, :-2]
    )
    fields = jnp.stack([pressure, conduct], 1)
    padded = padded_2(fields.astype(jnp.bfloat16), (("space", 2),), 1).astype(fields.dtype)
    press_low = padded[:, 0, 0]
    press_high = padded[:, 0, -1]
    cond_low = padded[:, 1, 0]
    cond_high = padded[:, 1, -1]
    press_below = jnp.concatenate([press_low[:, None], pressure[:, :-1]], 1)
    cond_below = jnp.concatenate([cond_low[:, None], conduct[:, :-1]], 1)
    press_above = jnp.concatenate([pressure[:, 1:], press_high[:, None]], 1)
    cond_above = jnp.concatenate([conduct[:, 1:], cond_high[:, None]], 1)
    lower_terms = face_term(conduct, cond_below, pressure, press_below)
    upper_terms = face_term(conduct, cond_above, pressure, press_above)
    flux_sum = flux_sum + lower_terms + upper_terms
    well_x = well_cells // (NY * NZ) - space_index * planes
    well_y = well_cells // NZ % NY
    well_z = well_cells % NZ
    onehot_x = (well_x[:, :, None] == jnp.arange(planes, dtype=jnp.int32)[None, None, :]).astype(
        jnp.float32
    ) * well_rates[:, :, None]
    onehot_y = (well_y[:, :, None] == jnp.arange(NY, dtype=jnp.int32)[None, None, :]).astype(
        jnp.float32
    )
    onehot_z = (well_z[:, :, None] == jnp.arange(NZ, dtype=jnp.int32)[None, None, :]).astype(
        jnp.float32
    )
    plane_rows = (onehot_x[:, :, :, None] * onehot_y[:, :, None, :]).reshape(
        batches, WELLS, planes * NY
    )
    source = jnp.einsum(
        "bwa,bwz->baz", plane_rows, onehot_z, precision=lax.Precision.HIGHEST
    ).reshape(batches, planes, NY, NZ)
    return flux_sum - source


def local_general(
    features,
    log_perm,
    well_cells,
    well_rates,
    lift_in,
    lift_out,
    spec_weight,
    point_weight,
    dec_in,
    dec_out,
):
    batches = features.shape[0]
    planes = features.shape[2]
    space_index = lax.axis_index("space")
    block = spec_weight.shape[1]
    cell_count = planes * NY * NZ
    z_forward, z_inverse = z_tables()
    y_forward = forward_table(NY, MY)
    y_inverse = inverse_table(NY, MY)
    x_forward = forward_table(NX, MX)
    x_inverse = inverse_table(NX, MX)
    perm_b = log_perm.astype(jnp.bfloat16).reshape(batches, 1, cell_count)
    lift_input = jnp.concatenate([features.reshape(batches, FIN, cell_count), perm_b], 1)
    lift_hidden = jnp.einsum("bfn,fh->bhn", lift_input, lift_in, preferred_element_type=jnp.float32)
    lifted = gelu_tanh(lift_hidden).astype(jnp.bfloat16)
    hidden_state = jnp.einsum(
        "bhn,hc->bcn", lifted, lift_out, preferred_element_type=jnp.float32
    ).astype(jnp.bfloat16)
    for layer_idx in range(LAYERS):
        zspec = jnp.dot(hidden_state.reshape(-1, NZ), z_forward, preferred_element_type=jnp.float32)
        zspec = zspec.astype(jnp.bfloat16).reshape(batches * C * planes, NY, 2, MZ)
        yz_spec = jnp.einsum(
            "aypk,ypqj->aqjk", zspec, y_forward, preferred_element_type=jnp.float32
        )
        yz_spec = yz_spec.astype(jnp.bfloat16).reshape(batches, C, planes, 2, MY * MZ)
        mode_weights = spec_weight[layer_idx].reshape(block, C, MX, 2, C)
        spectrum = jnp.einsum(
            "bcxpm,xpqi->bcqim",
            lax.all_to_all(yz_spec, "space", split_axis=4, concat_axis=2, tiled=True),
            x_forward,
            preferred_element_type=jnp.float32,
        ).astype(jnp.bfloat16)
        products = jnp.einsum(
            "bcqim,mcipo->bimqpo", spectrum, mode_weights, preferred_element_type=jnp.float32
        )
        real_part = products[:, :, :, 0, 0] - products[:, :, :, 1, 1]
        imag_part = products[:, :, :, 0, 1] + products[:, :, :, 1, 0]
        mixed_modes = jnp.stack([real_part, imag_part], 3).astype(jnp.bfloat16)
        back_field = jnp.einsum(
            "bimqo,iqpx->boxpm", mixed_modes, x_inverse, preferred_element_type=jnp.float32
        ).astype(jnp.bfloat16)
        returned = lax.all_to_all(back_field, "space", split_axis=2, concat_axis=4, tiled=True)
        returned = returned.reshape(batches * C * planes, 2, MY, MZ)
        y_back = jnp.einsum(
            "aqjk,jqpy->aypk", returned, y_inverse, preferred_element_type=jnp.float32
        ).astype(jnp.bfloat16)
        spectral = jnp.dot(
            y_back.reshape(-1, 2 * MZ), z_inverse, preferred_element_type=jnp.float32
        ).reshape(batches, C, cell_count)
        local_term = jnp.einsum(
            "bcn,co->bon", hidden_state, point_weight[layer_idx], preferred_element_type=jnp.float32
        )
        hidden_state = gelu_tanh(spectral + local_term).astype(jnp.bfloat16)
    decoded = gelu_tanh(
        jnp.einsum("bcn,cd->bdn", hidden_state, dec_in, preferred_element_type=jnp.float32)
    ).astype(jnp.bfloat16)
    decoded_out = jnp.einsum("bdn,de->ben", decoded, dec_out, preferred_element_type=jnp.float32)
    pressure = decoded_out[:, 0].reshape(batches, planes, NY, NZ)
    saturation = jax.nn.sigmoid(decoded_out[:, 1]).reshape(batches, planes, NY, NZ)
    states = jnp.stack([pressure, saturation], 1)
    conduct = mobility_of(saturation, log_perm)
    return (states, darcy(pressure, conduct, well_cells, well_rates))


BF = jnp.bfloat16
F32 = jnp.float32
PAIRS = NY // 2
PITCH = PAIRS + 8
MODE_STEP = 8
ROWS = 8
UNROLL = 4
LANES = 128


def np_waves(length, kept, one_sided):
    index = np.arange(kept)
    freqs = index if one_sided else np.where(index < kept // 2, index, length - kept + index)
    angles = (freqs[:, None] * np.arange(length)[None, :] % length) * (2.0 * math.pi / length)
    norm = 1.0 / math.sqrt(length)
    return np.cos(angles) * norm, np.sin(angles) * norm


def np_forward(length, kept):
    cosine, sine = np_waves(length, kept, False)
    return np.stack([np.stack([cosine.T, -sine.T], 1), np.stack([sine.T, cosine.T], 1)], 1)


def np_inverse(length, kept):
    cosine, sine = np_waves(length, kept, False)
    return np.stack([np.stack([cosine, sine], 1), np.stack([-sine, cosine], 1)], 1)


def by_plane(table, axis, count):
    planes = NX // count
    order = np.arange(NX).reshape(count, planes).T.reshape(-1)
    return np.take(table, order, axis)


def tables_for(count):
    own = MY // count
    cosine, sine = np_waves(NZ, MZ, True)
    twice = np.where(np.arange(MZ) == 0, 1.0, 2.0)[:, None]
    z_forward = np.concatenate([cosine.T, -sine.T], 1)
    z_inverse = np.concatenate([twice * cosine, -twice * sine], 0)
    y_forward = np_forward(NY, MY).reshape(PAIRS, 2, 2, 2, count, own)
    y_inverse = np_inverse(NY, MY).reshape(count, own, 2, 2, PAIRS, 2)
    pair = np.eye(2)
    tables = {
        "zf": np.kron(pair, z_forward),
        "zi": 0.5 * np.kron(pair, z_inverse),
        "yf": y_forward.transpose(3, 5, 4, 1, 2, 0).reshape(2 * MY, 2 * NY),
        "yi": y_inverse.transpose(5, 3, 4, 2, 1, 0).reshape(2 * NY, 2 * MY),
        "xf": by_plane(np_forward(NX, MX).transpose(1, 2, 3, 0).reshape(2, 2 * MX, NX), 2, count),
        "xi": by_plane(np_inverse(NX, MX).transpose(2, 3, 0, 1).reshape(2, NX, 2 * MX), 1, count),
    }
    return {name: jnp.asarray(table.astype(np.float32)).astype(BF) for name, table in tables.items()}


def dot32(a, b):
    return jnp.dot(a, b, preferred_element_type=F32)


def gelu_of_half(values):
    u = values.astype(BF)
    scale = math.sqrt(2.0 / math.pi)
    inner = u * (BF(2.0 * scale) + BF(8.0 * scale * 0.044715) * (u * u))
    return u + u * jnp.tanh(inner)


def swap_blocks(four):
    shape = four[0].shape
    lane = lax.broadcasted_iota(jnp.int32, shape, 1)
    low = lane < 64
    even = lane % 64 < 32
    a0, a1, a2, a3 = four

    def cross(a, b, keep, shift):
        return (
            jnp.where(keep, a, pltpu.roll(b, shift, 1)),
            jnp.where(keep, pltpu.roll(a, LANES - shift, 1), b),
        )

    b0, b2 = cross(a0, a2, low, 64)
    b1, b3 = cross(a1, a3, low, 64)
    c0, c1 = cross(b0, b1, even, 32)
    c2, c3 = cross(b2, b3, even, 32)
    return c0, c1, c2, c3


def send_plane(me, count, plane, send, recv, send_sem, recv_sem):
    for shift in range(1, count):
        target = lax.rem(me + shift, count)
        pltpu.make_async_remote_copy(
            src_ref=send.at[plane, target],
            dst_ref=recv.at[plane, me],
            send_sem=send_sem.at[plane],
            recv_sem=recv_sem.at[plane],
            device_id={"space": target},
            device_id_type=pl.DeviceIdType.MESH,
        ).start()
    recv[plane, me] = send[plane, me]


def wait_plane(count, plane, buffer, sem):
    part = buffer.at[plane, pl.ds(0, count - 1)]
    pltpu.make_async_copy(part, part, sem.at[plane]).wait()


def to_modes(plane, count, yf_ref, zs, flat, send):
    pieces = []
    for group in range(C // 4):
        four = [zs[(group * 4 + r) * PITCH : (group * 4 + r) * PITCH + PAIRS, :] for r in range(4)]
        pieces.append(jnp.concatenate([p.astype(BF) for p in swap_blocks(four)], 0))
    modes = dot32(yf_ref[...], jnp.concatenate(pieces, 1))
    tiles = C * MZ // LANES
    slots = 2 * MY // count * tiles
    for s in range(2 * MY // count):
        for t in range(tiles):
            flat[pl.ds(s * tiles + t, count, stride=slots), :] = modes[
                s * count : (s + 1) * count, t * LANES : (t + 1) * LANES
            ]
    send[plane] = flat[: count * slots, :].reshape(count, slots, LANES).astype(BF)


def lay_out(zs, start, values):
    for r in range(ROWS):
        zs[pl.ds(start + r, C, stride=PITCH), :] = values[r * C : (r + 1) * C, :]


def hid_rows(index):
    return pl.ds(pl.multiple_of(index * ROWS * C, ROWS * C), ROWS * C)


def lift_plane(plane, feat_ref, perm_ref, in_ref, lo_ref, zf_ref, hid, plain, xs, zs):
    for f in range(FIN + 1):
        plain[...] = perm_ref[0, plane] if f == FIN else feat_ref[0, f, plane].astype(F32)
        for y2 in range(2):
            xs[y2, pl.ds(f, PAIRS, stride=8), :] = plain[pl.ds(y2, PAIRS, stride=2), :]
    width = lo_ref.shape[1]

    def block(index, carry):
        start = pl.multiple_of(index * ROWS * 8, ROWS * 8)
        x = jnp.concatenate([xs[0, pl.ds(start, ROWS * 8), :], xs[1, pl.ds(start, ROWS * 8), :]], 1)
        lifted = gelu_of_half(dot32(in_ref[...], x.astype(BF)))
        parts = [
            dot32(lo_ref[...], lifted[r * width : (r + 1) * width, :]).astype(BF)
            for r in range(lifted.shape[0] // width)
        ]
        hidden = jnp.concatenate(parts, 0)
        hid[plane, hid_rows(index), :] = hidden
        lay_out(zs, index * ROWS, dot32(hidden, zf_ref[...]))
        return carry

    lax.fori_loop(0, PAIRS // ROWS, block, 0, unroll=UNROLL)


def from_modes(plane, count, recv, yi_ref, flat, zs):
    tiles = C * MZ // LANES
    slots = 2 * MY // count * tiles
    flat[: count * slots, :] = recv[plane].astype(F32).reshape(count * slots, LANES)
    rows = []
    for s in range(2 * MY // count):
        rows.append(
            jnp.concatenate(
                [flat[pl.ds(s * tiles + t, count, stride=slots), :] for t in range(tiles)], 1
            ).astype(BF)
        )
    back = dot32(yi_ref[...], jnp.concatenate(rows, 0))
    for group in range(C // 4):
        lanes = slice(group * LANES, (group + 1) * LANES)
        four = [back[g * PAIRS : (g + 1) * PAIRS, lanes] for g in range(4)]
        for r, piece in enumerate(swap_blocks(four)):
            zs[(group * 4 + r) * PITCH : (group * 4 + r) * PITCH + PAIRS, :] = piece


def layer_rows(plane, index, zs, hid, zi_ref, kp):
    start = index * ROWS
    parts = [zs[pl.ds(start + r, C, stride=PITCH), :].astype(BF) for r in range(ROWS)]
    spectral = dot32(jnp.concatenate(parts, 0), zi_ref[...])
    return gelu_of_half(spectral + dot32(kp, hid[plane, hid_rows(index), :]))


def middle_plane(plane, kp, zi_ref, zf_ref, hid, zs, zs2):
    def block(index, carry):
        hidden = layer_rows(plane, index, zs, hid, zi_ref, kp)
        hid[plane, hid_rows(index), :] = hidden
        lay_out(zs2, index * ROWS, dot32(hidden, zf_ref[...]))
        return carry

    lax.fori_loop(0, PAIRS // ROWS, block, 0, unroll=UNROLL)


def final_plane(plane, kp, zi_ref, di_ref, do_ref, perm_ref, hid, zs, st_ref, cond_ref):
    def block(index, carry):
        hidden = layer_rows(plane, index, zs, hid, zi_ref, kp)
        both = dot32(do_ref[...], gelu_of_half(dot32(di_ref[...], hidden)))
        for y2 in range(2):
            lanes = slice(y2 * NZ, (y2 + 1) * NZ)
            where = pl.ds(index * ROWS * 2 + y2, ROWS, stride=2)
            st_ref[0, 0, plane, where, :] = both[:ROWS, lanes]
            st_ref[0, 1, plane, where, :] = both[ROWS:, lanes]
        return carry

    lax.fori_loop(0, PAIRS // ROWS, block, 0, unroll=UNROLL)
    sat = jax.nn.sigmoid(st_ref[0, 1, plane])
    st_ref[0, 1, plane] = sat
    cond_ref[0, plane] = mobility_of(sat, perm_ref[0, plane])


def mix_modes(planes, count, recv, send, wbuf, xf_ref, xi_ref, flat, spec, mixed, turned, rhs):
    own = MY // count
    tiles = C * MZ // LANES
    slots = 2 * own * tiles
    every = count * planes
    wide = MX * 2 * C
    for plane in range(planes):
        flat[plane * count * slots : (plane + 1) * count * slots, :] = (
            recv[plane].astype(F32).reshape(count * slots, LANES)
        )
    total = 0.0
    for p in range(2):
        right = jnp.concatenate(
            [
                flat[pl.ds(p * own * tiles + t, every, stride=slots), :].astype(BF)
                for t in range(own * tiles)
            ],
            1,
        )
        total = total + dot32(xf_ref[p], right)
    spec[:, : 2 * MX] = total.T
    chunk = 512

    def step(index, carry):
        first = pl.multiple_of(index * MODE_STEP, MODE_STEP)
        base = first // MZ * (C * MZ) + first % MZ
        rows = [spec[pl.ds(base + r, C, stride=MZ), :] for r in range(MODE_STEP)]
        values = jnp.concatenate(rows, 0)[:, : 2 * MX].astype(BF)
        for piece in range(wide // chunk):
            lo = piece * chunk
            row = lax.broadcasted_iota(jnp.int32, (2 * MX, chunk), 0)
            col = lax.broadcasted_iota(jnp.int32, (2 * MX, chunk), 1) + lo
            weights = wbuf[pl.ds(first, MODE_STEP), :, lo : lo + chunk]
            weights = weights.reshape(MODE_STEP * C, chunk).astype(F32)
            sums = []
            for q in range(2):
                pick = jnp.where(row == col // (2 * C) + q * MX, 1.0, 0.0).astype(BF)
                terms = dot32(values, pick) * weights
                sums.append(jnp.sum(terms.reshape(MODE_STEP, C, chunk), 1))
            lane = lax.broadcasted_iota(jnp.int32, (MODE_STEP, chunk), 1)
            turn = jnp.where(
                lane % (2 * C) < C, -pltpu.roll(sums[1], chunk - C, 1), pltpu.roll(sums[1], C, 1)
            )
            mixed[pl.ds(first, MODE_STEP), lo : lo + chunk] = sums[0] + turn
        return carry

    lax.fori_loop(0, own * MZ // MODE_STEP, step, 0)
    turned[:, : own * MZ] = mixed[...].T
    for o in range(C):
        piece = turned[pl.ds(o, 2 * MX, stride=C), :]
        for jj in range(own):
            lo = (jj * C + o) * MZ
            rhs[:, lo : lo + MZ] = piece[:, jj * MZ : (jj + 1) * MZ]
    right = rhs[...].astype(BF)
    for p in range(2):
        back = dot32(xi_ref[p], right)
        for t in range(own * tiles):
            flat[pl.ds(p * own * tiles + t, every, stride=slots), :] = back[
                :, t * LANES : (t + 1) * LANES
            ]
    for plane in range(planes):
        send[plane] = (
            flat[plane * count * slots : (plane + 1) * count * slots, :]
            .reshape(count, slots, LANES)
            .astype(BF)
        )


def whole_kernel(
    planes, count, feat_ref, perm_ref, lift_in, lift_out, point, dec_in, dec_out, zf_ref, zi_ref,
    yf_ref, yi_ref, xf_ref, xi_ref, w_hbm, st_ref, cond_ref,
    hid, wbuf, send_f, recv_f, send_b, recv_b, flat, spec, mixed, turned, rhs, zs, zs2, xs, plain,
    in_ref, lo_ref, kp_ref, di_ref, do_ref, w_sem, sf_sem, rf_sem, sb_sem, rb_sem,
):
    me = lax.axis_index("space")
    barrier = pltpu.get_barrier_semaphore()
    for shift in range(1, count):
        pl.semaphore_signal(
            barrier,
            inc=1,
            device_id={"space": lax.rem(me + shift, count)},
            device_id_type=pl.DeviceIdType.MESH,
        )
    fetch = pltpu.make_async_copy(w_hbm.at[0], wbuf, w_sem.at[0])
    fetch.start()
    xs[...] = jnp.zeros_like(xs)
    in_ref[...] = diag_of(lift_in[...], ROWS, 8, 0.5)
    lo_ref[...] = diag_of(lift_out[...], 2, lift_out.shape[0], 1.0)
    for layer in range(LAYERS):
        kp_ref[layer] = diag_of(point[layer], ROWS, C, 0.5)
    di_ref[...] = diag_of(dec_in[...], ROWS, C, 0.5)
    dec = dec_out.shape[0]
    do_ref[...] = spread(
        dec_out[...],
        2 * ROWS,
        ROWS * dec,
        lambda i: i // ROWS,
        lambda j: j % dec,
        lambda i, j: i % ROWS == j // dec,
        1.0,
    )
    pl.semaphore_wait(barrier, count - 1)

    def over(body):
        def run(plane, carry):
            body(plane)
            return carry

        lax.fori_loop(0, planes, run, 0)

    def lift(plane):
        lift_plane(plane, feat_ref, perm_ref, in_ref, lo_ref, zf_ref, hid, plain, xs, zs)
        to_modes(plane, count, yf_ref, zs, flat, send_f)
        send_plane(me, count, plane, send_f, recv_f, sf_sem, rf_sem)

    over(lift)
    for layer in range(LAYERS):
        fetch.wait()
        over(lambda plane: wait_plane(count, plane, recv_f, rf_sem))
        over(lambda plane: wait_plane(count, plane, send_f, sf_sem))
        mix_modes(
            planes, count, recv_f, send_b, wbuf, xf_ref, xi_ref, flat, spec, mixed, turned, rhs
        )
        if layer + 1 < LAYERS:
            fetch = pltpu.make_async_copy(w_hbm.at[layer + 1], wbuf, w_sem.at[layer + 1])
            fetch.start()
        over(lambda plane: send_plane(me, count, plane, send_b, recv_b, sb_sem, rb_sem))

        def rest(plane):
            wait_plane(count, plane, recv_b, rb_sem)
            from_modes(plane, count, recv_b, yi_ref, flat, zs)
            if layer + 1 < LAYERS:
                middle_plane(plane, kp_ref[layer], zi_ref, zf_ref, hid, zs, zs2)
                to_modes(plane, count, yf_ref, zs2, flat, send_f)
                send_plane(me, count, plane, send_f, recv_f, sf_sem, rf_sem)
            else:
                final_plane(
                    plane, kp_ref[layer], zi_ref, di_ref, do_ref, perm_ref, hid, zs, st_ref, cond_ref
                )

        over(rest)
        over(lambda plane: wait_plane(count, plane, send_b, sb_sem))


def ones_where(shape, test, value=1.0):
    row = lax.broadcasted_iota(jnp.int32, shape, 0)
    col = lax.broadcasted_iota(jnp.int32, shape, 1)
    return jnp.where(test(row, col), value, 0.0)


def spread(matrix, rows, cols, row_of, col_of, keep, value):
    take = ones_where((rows, matrix.shape[1]), lambda i, j: row_of(i) == j).astype(BF)
    put = ones_where((matrix.shape[0], cols), lambda i, j: col_of(j) == i).astype(BF)
    part = lax.dot_general(take, matrix, (((1,), (1,)), ((), ())), preferred_element_type=F32)
    return (dot32(part.astype(BF), put) * ones_where((rows, cols), keep, value)).astype(BF)


def diag_of(matrix, copies, width, value):
    depth, height = matrix.shape
    return spread(
        matrix,
        copies * height,
        copies * width,
        lambda i: i % height,
        lambda j: j % width,
        lambda i, j: i // height == j // width,
        value,
    )


def local_fast(
    features,
    log_perm,
    well_cells,
    well_rates,
    lift_in,
    lift_out,
    spec_weight,
    point_weight,
    dec_in,
    dec_out,
):
    planes = features.shape[2]
    count = lax.axis_size("space")
    own = MY // count
    modes = own * MZ
    slots = 2 * modes * C // LANES
    tables = tables_for(count)
    lift, dec = lift_in.shape[1], dec_in.shape[1]
    operands = (
        features,
        log_perm,
        lift_in,
        lift_out,
        point_weight,
        dec_in,
        dec_out,
    ) + tuple(tables[name] for name in ("zf", "zi", "yf", "yi", "xf", "xi"))
    vmem = pl.BlockSpec(memory_space=pltpu.VMEM)
    exchange = pltpu.VMEM((planes, count, slots, LANES), BF)
    states, conduct = pl.pallas_call(
        lambda *refs: whole_kernel(planes, count, *refs),
        in_specs=[vmem] * len(operands) + [pl.BlockSpec(memory_space=pl.ANY)],
        out_specs=[vmem, vmem],
        out_shape=[
            jax.ShapeDtypeStruct((1, 2, planes, NY, NZ), F32),
            jax.ShapeDtypeStruct((1, planes, NY, NZ), F32),
        ],
        scratch_shapes=[
            pltpu.VMEM((planes, PAIRS * C, 2 * NZ), BF),
            pltpu.VMEM(spec_weight.shape[1:], BF),
            exchange,
            exchange,
            exchange,
            exchange,
            pltpu.VMEM((planes * count * slots, LANES), F32),
            pltpu.VMEM((modes * C, LANES), F32),
            pltpu.VMEM((modes, MX * 2 * C), F32),
            pltpu.VMEM((MX * 2 * C, LANES), F32),
            pltpu.VMEM((2 * MX, modes * C), F32),
            pltpu.VMEM((C * PITCH, LANES), F32),
            pltpu.VMEM((C * PITCH, LANES), F32),
            pltpu.VMEM((2, PAIRS * 8, NZ), F32),
            pltpu.VMEM((NY, NZ), F32),
            pltpu.VMEM((ROWS * lift, ROWS * 8), BF),
            pltpu.VMEM((2 * C, 2 * lift), BF),
            pltpu.VMEM((LAYERS, ROWS * C, ROWS * C), BF),
            pltpu.VMEM((ROWS * dec, ROWS * C), BF),
            pltpu.VMEM((2 * ROWS, ROWS * dec), BF),
            pltpu.SemaphoreType.DMA((LAYERS,)),
        ]
        + [pltpu.SemaphoreType.DMA((planes,))] * 4,
        compiler_params=pltpu.CompilerParams(
            collective_id=0, has_side_effects=True, vmem_limit_bytes=60 * 1024 * 1024
        ),
        name="whole",
    )(*operands, spec_weight)
    return (states, darcy(states[:, 0], conduct, well_cells, well_rates))


def local(features, log_perm, well_cells, well_rates, lift_in, lift_out, spec_weight, *rest):
    batches, planes = features.shape[0], features.shape[2]
    count = lax.axis_size("space")
    fits = batches == 1 and planes == 8 and count % 8 == 0 and MY % count == 0
    run = local_fast if fits else local_general
    return run(
        features, log_perm, well_cells, well_rates, lift_in, lift_out, spec_weight, *rest
    )


def solution(mesh):
    return jax.shard_map(
        local,
        mesh=mesh,
        in_specs=(
            P("sample", None, "space", None, None),
            P("sample", "space", None, None),
            P("sample", None),
            P("sample", None),
            P(),
            P(),
            P(None, "space", None, None),
            P(),
            P(),
            P(),
        ),
        out_specs=(P("sample", None, "space", None, None), P("sample", "space", None, None)),
        check_vma=False,
    )
```
